128 devices in a mesh: face: 4 (over y), tile: 32 (over x, z, core).
Axes of the slice: x: 4, y: 4, z: 4, core: 2. Of those that a mesh axis runs over, the one named last changes fastest.
Arguments:
- latlon: bfloat16 [8192, 74, 128], P(('face', 'tile')), may hold values from -6 to 6
- intersection_weight: bfloat16 [8192, 4, 128, 128], P(('face', 'tile')), may hold values from -0.5 to 0.5
- target_dev: int32 [8192, 4], P(('face', 'tile')), may hold values from 0 to 127, all different within a row; in each aligned block of 64 rows (0 to 63, 64 to 127, ...) at most 2 rows name the same one
- target_piece: int32 [8192, 4], P(('face', 'tile')), may hold values from 0 to 63
- counts: int32 [8192], P(('face', 'tile')), may hold values from 1 to 4
- conv_weight: bfloat16 [9, 256, 74], replicated, may hold values from -0.25 to 0.25
- cotangent: bfloat16 [4, 256, 512, 512], P('face', None, 'tile'), may hold values from -6 to 6
Outputs:
- activation: bfloat16 [4, 256, 512, 512], P('face', None, 'tile')
- grad_conv: float32 [9, 256, 74], replicated
- grad_latlon: bfloat16 [8192, 74, 128], P(('face', 'tile'))
The draws below stay inside these ranges and needn't reach their ends.
Inputs may be any that keep to these rules, and one draw needn't show every extreme that they name: `target_dev`: among the 4 entries of one block all owners differ; among the entries of one device's 64 blocks (aligned blocks of rows) no owner is named more than 2 times, a bound that some block reaches. Entries j >= counts[b] of block b are not live.
All inputs are finite; a program needn't handle non-finite values.
Results may differ from the reference program's by a relative error of at most 0.0091.
Values may be sent and summed in bfloat16 or wider, within the bound.
A program may use at most 192 MiB of HBM per device.

```python
import math
import jax
import jax.numpy as jnp
import numpy as np
from jax import lax

C = 74
HID = 256
ROWS = 16
COLS = 512
PP = 128
BP = 128
K = 4
NB_DEV = 64
NB = 8192
PIECES = 64
CAP = 2
SIDE = 512
FACES = 4
N_FACE = 4
N_TILE = 32


def touch_ends(drawn, stream_key, least, high):
    longest = drawn.shape.index(max(drawn.shape))
    spots = []
    for shift in (0, 1):
        where = [jax.random.randint(jax.random.fold_in(stream_key, axis), (), 0, length) for axis, length in enumerate(drawn.shape)]
        where[longest] = (where[longest] + shift) % drawn.shape[longest]
        spots.append(tuple(where))
    return drawn.at[spots[0]].set(least).at[spots[1]].set(high)


def level_of(rng, dims, shards, low, top_value):
    def one(position, blocks):
        heights = jax.random.uniform(jax.random.fold_in(jax.random.fold_in(rng, 6), position), (blocks,), jnp.float32, low / len(shards), top_value / len(shards))
        return jnp.repeat(jnp.exp(heights), dims[position] // blocks).reshape((-1,) + (1,) * (len(dims) - position - 1))

    gain = one(*shards[0])
    for cut in shards[1:]:
        gain = gain * one(*cut)
    return gain


def shared_out(rng, own, number, rows, count, top, limit, skew):
    ranking = jax.random.permutation(rng, count)
    packed, ordinary = load_shares(count, rows * top, limit, skew, True), load_shares(count, rows * top, limit, skew, False)
    places = jnp.arange(count)

    def named(tallies, turn):
        used = int((tallies > 0).sum())
        fixed = max(1, used // 4)
        passed = fixed + (places - fixed + turn * (used - fixed)) % max(1, count - fixed)
        return jnp.zeros((count,), jnp.int32).at[ranking[jnp.where(places < fixed, places, passed)]].set(jnp.asarray(tallies, jnp.int32))

    tallies = jnp.where(number % 4 == 0, named(packed, number // 4), named(ordinary, number - number // 4 - 1))
    mixed = jax.random.permutation(jax.random.fold_in(own, 3), count)
    source_of, receiver = mixed[0:count // 2 * 2:2], mixed[1:count // 2 * 2:2]
    slack = jnp.minimum(tallies[source_of] - 1, limit - tallies[receiver]) // 2
    slack = jnp.where((source_of == ranking[0]) | (receiver == ranking[0]) | (tallies[receiver] == 0), 0, jnp.maximum(slack, 0))
    passed = jax.random.randint(jax.random.fold_in(own, 4), (count // 2,), 0, 1 << 20) % (slack + 1)
    tallies = tallies.at[source_of].add(-passed).at[receiver].add(passed)
    items = jnp.searchsorted(jnp.cumsum(tallies), jnp.arange(rows * top), side="right").astype(jnp.int32)
    grid = items.reshape(top, rows).T
    grid = grid[jax.random.permutation(jax.random.fold_in(own, 1), rows)]
    turn = jax.random.randint(jax.random.fold_in(own, 2), (rows, 1), 0, top)
    return jnp.take_along_axis(grid, (jnp.arange(top)[None, :] + turn) % top, axis=1)


def load_shares(number_of, total, most, lean, full):
    portions = [(1 << 20) // math.isqrt(rank ** lean) + 1 for rank in range(1, number_of + 1)]
    largest = most if full else min(most, max(-(-total // number_of), total * portions[0] // sum(portions)))
    least = 1 if total - largest >= number_of - 1 else 0
    given, spare = [largest] + [least] * (number_of - 1), total - largest - least * (number_of - 1)
    while spare > 0:
        candidates = [i for i in range(1, number_of) if given[i] < largest] or [i for i in range(1, number_of) if given[i] < most]
        mass, left = sum([portions[i] for i in candidates]), spare
        for i in candidates:
            more = min(most - given[i], max(1, left * portions[i] // mass), spare)
            given[i] = given[i] + more
            spare = spare - more
    return np.array(given)


def noise(own_key, extent, scale, most, cuts=(), kind=jnp.bfloat16):
    drawn = jax.random.normal(own_key, extent, jnp.float32) * scale
    if len(cuts) > 0:
        drawn = level_of(own_key, extent, cuts, -0.22, 0.18) * drawn
    return jnp.clip(drawn, min=-most, max=most).astype(kind)


def setup_inputs(seed: int = 0) -> dict:
    key_list = jax.random.split(jax.random.key(seed), 8)
    latlon = noise(key_list[0], (NB, C, BP), 1.0, 6.0, ((0, 128),))
    intersection_weight = noise(key_list[1], (NB, K, BP, PP), BP ** -0.5, 0.5, ((0, 128),))
    target_dev_keys = jax.random.split(jax.random.fold_in(key_list[2], 1), NB // NB_DEV)
    target_dev_turns = jax.random.permutation(jax.random.fold_in(key_list[2], 3), NB // NB_DEV)
    target_dev = jax.vmap(lambda own, number: shared_out(jax.random.fold_in(key_list[2], 2), own, number, NB_DEV, N_FACE * N_TILE, K, CAP, 2))(target_dev_keys, target_dev_turns).reshape((NB, K))
    target_piece = touch_ends(jax.random.randint(key_list[3], (NB, K), 0, PIECES), jax.random.fold_in(key_list[3], 1), 0, PIECES - 1).astype(jnp.int32)
    counts = touch_ends(jax.random.randint(key_list[4], (NB,), 1, K + 1), jax.random.fold_in(key_list[4], 1), 1, K).astype(jnp.int32)
    conv_weight = noise(key_list[5], (9, HID, C), (9 * C) ** -0.5, 0.25)
    cotangent = noise(key_list[6], (FACES, HID, SIDE, COLS), 1.0, 6.0, ((0, 4), (2, 32)))
    return dict(latlon=latlon, intersection_weight=intersection_weight, target_dev=target_dev, target_piece=target_piece, counts=counts, conv_weight=conv_weight, cotangent=cotangent)


def gelu_parts(value):
    inner = 0.7978845608 * (value + 0.044715 * value * value * value)
    tanh_part = jnp.tanh(inner)
    result = 0.5 * value * (1.0 + tanh_part)
    slope = 0.5 * (1.0 + tanh_part) + 0.5 * value * (1.0 - tanh_part * tanh_part) * 0.7978845608 * (1.0 + 0.134145 * value * value)
    return (result, slope)

def cycle_pad(array):
    padded = jnp.pad(array, ((0, 0), (1, 1), (0, 0)))
    return jnp.concatenate([padded[:, :, -1:], padded, padded[:, :, :1]], axis=2)

def to_cycle(array):
    return array.transpose(1, 2, 0, 3).reshape(array.shape[1], array.shape[2], array.shape[0] * array.shape[3])

def from_cycle(array):
    return array.reshape(array.shape[0], array.shape[1], N_FACE, COLS).transpose(2, 0, 1, 3)

def reference(latlon, intersection_weight, target_dev, target_piece, counts, conv_weight, cotangent):
    devices = N_FACE * N_TILE
    blocks = latlon.shape[0] // devices
    live = (jnp.arange(K, dtype=jnp.int32)[None, :] < counts[:, None]).astype(jnp.float32)
    dest = (target_dev * PIECES + target_piece).astype(jnp.int32)
    groups = (latlon.reshape(devices, blocks, C, BP), intersection_weight.reshape(devices, blocks, K, BP, PP), dest.reshape(devices, blocks, K), live.reshape(devices, blocks, K))

    def regrid(field_sum, items):
        lat, weights, targets, alive = items
        part = jnp.einsum('bcp,bjpq->bjcq', lat.astype(jnp.float32), weights.astype(jnp.float32)) * alive[:, :, None, None]
        part = lax.optimization_barrier(part.astype(jnp.bfloat16)).astype(jnp.float32)
        field_sum = field_sum.at[targets.reshape(-1)].add(part.reshape(-1, C, PP))
        return (field_sum, None)
    field_sum, unused = lax.scan(regrid, jnp.zeros((devices * PIECES, C, PP), jnp.float32), groups)
    field = field_sum.astype(jnp.bfloat16).reshape(N_FACE, N_TILE, PIECES, C, PP).transpose(0, 3, 1, 2, 4)
    field = field.reshape(N_FACE, C, N_TILE * ROWS, COLS)
    cycle = N_FACE * COLS
    field_pad = cycle_pad(to_cycle(field))
    cot_cycle = to_cycle(cotangent)
    kernel = conv_weight.astype(jnp.float32)

    def band(grad_sum, tile):
        window = lax.dynamic_slice_in_dim(field_pad, tile * ROWS, ROWS + 2, axis=1).astype(jnp.float32)
        cot = lax.dynamic_slice_in_dim(cot_cycle, tile * ROWS, ROWS, axis=1).astype(jnp.float32)
        pre = jnp.zeros((HID, ROWS, cycle), jnp.float32)
        for k in range(9):
            ky, kx = divmod(k, 3)
            pre = pre + jnp.einsum('oc,crw->orw', kernel[k], window[:, ky:ky + ROWS, kx:kx + cycle])
        result, slope = gelu_parts(pre)
        dpre = (cot * slope).astype(jnp.bfloat16)
        dpre_f = lax.optimization_barrier(dpre).astype(jnp.float32)
        terms = []
        for k in range(9):
            ky, kx = divmod(k, 3)
            terms.append(jnp.einsum('orw,crw->oc', dpre_f, window[:, ky:ky + ROWS, kx:kx + cycle]))
        return (grad_sum + jnp.stack(terms), (result.astype(jnp.bfloat16), dpre))
    grad_sum, outs = lax.scan(band, jnp.zeros((9, HID, C), jnp.float32), jnp.arange(N_TILE, dtype=jnp.int32))
    act_bands, dpre_bands = outs
    activation = from_cycle(act_bands.transpose(1, 0, 2, 3).reshape(HID, N_TILE * ROWS, cycle))
    dpre_pad = cycle_pad(dpre_bands.transpose(1, 0, 2, 3).reshape(HID, N_TILE * ROWS, cycle))

    def back(carry, tile):
        window = lax.dynamic_slice_in_dim(dpre_pad, tile * ROWS, ROWS + 2, axis=1).astype(jnp.float32)
        total = jnp.zeros((C, ROWS, cycle), jnp.float32)
        for k in range(9):
            ky, kx = divmod(k, 3)
            total = total + jnp.einsum('oc,orw->crw', kernel[k], window[:, 2 - ky:2 - ky + ROWS, 2 - kx:2 - kx + cycle])
        return (carry, total.astype(jnp.bfloat16))
    unused, dbands = lax.scan(back, jnp.zeros((), jnp.float32), jnp.arange(N_TILE, dtype=jnp.int32))
    dfield = from_cycle(dbands.transpose(1, 0, 2, 3).reshape(C, N_TILE * ROWS, cycle))
    dfield = dfield.reshape(N_FACE, C, N_TILE, ROWS * COLS).transpose(0, 2, 1, 3)
    dfield = dfield.reshape(devices, C, PIECES, PP).transpose(0, 2, 1, 3).reshape(devices * PIECES, C, PP)

    def unregrid(carry, items):
        lat, weights, targets, alive = items
        got = dfield[targets].astype(jnp.float32) * alive[:, :, None, None]
        grad = jnp.einsum('bjcq,bjpq->bcp', got, weights.astype(jnp.float32))
        return (carry, grad.astype(jnp.bfloat16))
    unused, grad_lat = lax.scan(unregrid, jnp.zeros((), jnp.float32), groups)
    grad_latlon = grad_lat.reshape(devices * blocks, C, BP)
    grad_conv = grad_sum * (1.0 / math.sqrt(N_FACE * N_TILE * ROWS * COLS))
    return (activation, grad_conv, grad_latlon)
```

```python
import functools
import math

import jax
import jax.numpy as jnp
from jax import lax
from jax.experimental import pallas as pl
from jax.experimental.pallas import tpu as pltpu
from jax.sharding import PartitionSpec as P

C = 74
CP = 80
SL = 76
HID = 256
ROWS = 16
COLS = 512
WIDE = 640
PP = 128
K = 4
PIECES = 64
DEVS = 128
GRP = 8
VMEM_LIMIT = 63 * 1024 * 1024
MESH = pl.DeviceIdType.MESH
f32 = jnp.float32
bf16 = jnp.bfloat16


def params(**kw):
    return pltpu.CompilerParams(vmem_limit_bytes=VMEM_LIMIT, **kw)


def whole(shape):
    zeros = (0,) * len(shape)
    return pl.BlockSpec(shape, lambda *a: zeros)


def partial_kernel(key_ref, lat_ref, w_ref, out_ref):
    step = pl.program_id(0)
    for g in range(GRP):
        parts = []
        for s in range(2):
            key = key_ref[(step * GRP + g) * 2 + s]
            entry = key >> 7
            alive = (key & 1).astype(f32)
            piece = ((key >> 1) & 63).astype(f32)
            value = jnp.dot(lat_ref[entry >> 2], w_ref[entry], preferred_element_type=f32)
            parts += [value * alive, jnp.full((SL - C, PP), piece, f32)]
        out_ref[g] = jnp.concatenate(parts, axis=0).astype(bf16)


def partial_products(keys, lat, weight):
    return pl.pallas_call(
        partial_kernel,
        grid_spec=pltpu.PrefetchScalarGridSpec(
            num_scalar_prefetch=1,
            grid=(DEVS // GRP,),
            in_specs=[whole(lat.shape), whole(weight.shape)],
            out_specs=pl.BlockSpec((GRP, 2 * SL, PP), lambda i, *a: (i, 0, 0)),
        ),
        out_shape=jax.ShapeDtypeStruct((DEVS, 2 * SL, PP), bf16),
        compiler_params=params(),
        name="partial",
    )(keys, lat, weight)


def gather_kernel(piece_ref, recv_ref, field_ref, pack_ref, acc_ref):
    step = pl.program_id(0)

    @pl.when(step == 0)
    def _():
        acc_ref[...] = jnp.zeros_like(acc_ref)

    for g in range(GRP):
        block = recv_ref[g].astype(f32)
        for s in range(2):
            piece = piece_ref[(step * GRP + g) * 2 + s]
            acc_ref[piece, :SL] += block[s * SL : (s + 1) * SL]

    @pl.when(step == pl.num_programs(0) - 1)
    def _():
        real = lax.broadcasted_iota(jnp.int32, (CP, PP), 0) < C
        lane = lax.broadcasted_iota(jnp.int32, (CP, PP), 1)
        left = jnp.zeros((CP, PP), f32)
        right = jnp.zeros((CP, PP), f32)
        for r in range(ROWS):
            for i in range(4):
                tile = jnp.where(real, acc_ref[r * 4 + i], 0.0)
                field_ref[r * 4 + i] = tile.astype(bf16)
                mine = (lane >> 1) == r
                if i == 0:
                    left = jnp.where(mine, pltpu.roll(tile, 2 * r, 1) if r else tile, left)
                if i == 3:
                    right = jnp.where(mine, pltpu.roll(tile, 2 * r + 2, 1), right)
        pack_ref[0] = left.astype(bf16)
        pack_ref[1] = right.astype(bf16)


def gather_field(pieces, recv):
    return pl.pallas_call(
        gather_kernel,
        grid_spec=pltpu.PrefetchScalarGridSpec(
            num_scalar_prefetch=1,
            grid=(DEVS // GRP,),
            in_specs=[pl.BlockSpec((GRP, 2 * SL, PP), lambda i, *a: (i, 0, 0))],
            out_specs=[whole((PIECES, CP, PP)), whole((2, CP, PP))],
            scratch_shapes=[pltpu.VMEM((PIECES, CP, PP), f32)],
        ),
        out_shape=[
            jax.ShapeDtypeStruct((PIECES, CP, PP), bf16),
            jax.ShapeDtypeStruct((2, CP, PP), bf16),
        ],
        compiler_params=params(),
        name="gather_field",
    )(pieces, recv)


def halo_kernel(field_ref, pack_ref, top_ref, bottom_ref, side_ref, send_sem, recv_sem):
    face = lax.axis_index("face")
    tile = lax.axis_index("tile")

    def at(df, dt):
        return (lax.rem(face + df + 4, 4), lax.rem(tile + dt + 32, 32))

    plan = [
        (field_ref.at[pl.ds(56, 8)], top_ref, at(0, 1)),
        (field_ref.at[pl.ds(0, 8)], bottom_ref, at(0, -1)),
    ]
    for dt in (-1, 0, 1):
        plan.append((pack_ref.at[1], side_ref.at[1 - dt], at(1, dt)))
        plan.append((pack_ref.at[0], side_ref.at[4 - dt], at(-1, dt)))
    barrier = pltpu.get_barrier_semaphore()
    for _, _, to in plan:
        pl.semaphore_signal(barrier, inc=1, device_id=to, device_id_type=MESH)
    pl.semaphore_wait(barrier, len(plan))
    copies = [
        pltpu.make_async_remote_copy(
            src_ref=src,
            dst_ref=dst,
            send_sem=send_sem.at[i],
            recv_sem=recv_sem.at[i],
            device_id=to,
            device_id_type=MESH,
        )
        for i, (src, dst, to) in enumerate(plan)
    ]
    for copy in copies:
        copy.start()
    for copy in copies:
        copy.wait()


def halo(field, pack):
    vmem = pl.BlockSpec(memory_space=pltpu.VMEM)
    return pl.pallas_call(
        halo_kernel,
        in_specs=[vmem, vmem],
        out_specs=[vmem, vmem, vmem],
        out_shape=[
            jax.ShapeDtypeStruct((8, CP, PP), bf16),
            jax.ShapeDtypeStruct((8, CP, PP), bf16),
            jax.ShapeDtypeStruct((6, CP, PP), bf16),
        ],
        scratch_shapes=[pltpu.SemaphoreType.DMA((8,)), pltpu.SemaphoreType.DMA((8,))],
        compiler_params=pltpu.CompilerParams(collective_id=0, has_side_effects=True),
        name="halo",
    )(field, pack)


def conv_kernel(
    meta_ref, field_ref, top_ref, bottom_ref, side_ref, wf_ref, wb_ref, cot_ref,
    act_ref, grad_ref, dfield_ref, x_ref, d_ref, pre_ref,
):
    step = pl.program_id(0)

    @pl.when(step == 0)
    def _():
        tile_at = meta_ref[0]
        has_top = (tile_at != 0).astype(f32)
        has_bottom = (tile_at != 31).astype(f32)
        lane = lax.broadcasted_iota(jnp.int32, (CP, PP), 1)

        def row(q, tiles, lefts, rights, at, factor):
            ext_l = pltpu.roll(lefts, (254 - 2 * at) % 128, 1) if 2 * at != 126 else lefts
            ext_r = pltpu.roll(rights, (128 - 2 * at) % 128, 1) if at else rights
            ext = jnp.where(lane < 2, ext_r, jnp.where(lane >= 126, ext_l, 0.0))
            full = jnp.concatenate(tiles + [ext], axis=1)
            if factor is not None:
                full = full * factor
            x_ref[q, 0:CP] = pltpu.roll(full, 1, 1).astype(bf16)
            x_ref[q, CP : 2 * CP] = full.astype(bf16)
            x_ref[q, 2 * CP : 3 * CP] = pltpu.roll(full, WIDE - 1, 1).astype(bf16)

        sides = [side_ref[i].astype(f32) for i in range(6)]
        for q in range(20):
            if q < 2:
                tiles = [top_ref[q * 4 + i].astype(f32) for i in range(4)]
                row(q, tiles, sides[0], sides[3], 14 + q, has_top)
            elif q < 18:
                tiles = [field_ref[(q - 2) * 4 + i].astype(f32) for i in range(4)]
                row(q, tiles, sides[1], sides[4], q - 2, None)
            else:
                tiles = [bottom_ref[(q - 18) * 4 + i].astype(f32) for i in range(4)]
                row(q, tiles, sides[2], sides[5], q - 18, has_bottom)
        grad_ref[...] = jnp.zeros_like(grad_ref)

    total = jnp.dot(wf_ref[0], x_ref[step], preferred_element_type=f32)
    total += jnp.dot(wf_ref[1], x_ref[step + 1], preferred_element_type=f32)
    total += jnp.dot(wf_ref[2], x_ref[step + 2], preferred_element_type=f32)
    pre_ref[...] = total
    for at in range(0, HID, 32):
        v = pre_ref[at : at + 32]
        square = v * v
        t = jnp.tanh(v * (0.7978845608 + (0.7978845608 * 0.044715) * square))
        half = 0.5 + 0.5 * t
        result = v * half
        slope = half + result * (1.0 - t) * (0.7978845608 + (0.7978845608 * 0.134145) * square)

        @pl.when((step >= 1) & (step <= ROWS))
        def _():
            act_ref[0, at : at + 32] = result[:, :COLS].astype(bf16)

        d_ref[step, at : at + 32] = (cot_ref[0, at : at + 32].astype(f32) * slope).astype(bf16)

    @pl.when((step >= 1) & (step <= ROWS))
    def _():
        dpre = d_ref[step][:, :COLS]
        for ky in range(3):
            grad_ref[ky] += lax.dot_general(
                x_ref[step + ky][:, :COLS], dpre, (((1,), (1,)), ((), ())),
                preferred_element_type=f32,
            )

    @pl.when(step >= 2)
    def _():
        back = jnp.dot(wb_ref[0], d_ref[step], preferred_element_type=f32)
        back += jnp.dot(wb_ref[1], d_ref[step - 1], preferred_element_type=f32)
        back += jnp.dot(wb_ref[2], d_ref[step - 2], preferred_element_type=f32)
        out = (
            pltpu.roll(back[0:CP], WIDE - 1, 1)
            + back[CP : 2 * CP]
            + pltpu.roll(back[2 * CP : 3 * CP], 1, 1)
        )
        for i in range(4):
            dfield_ref[i] = out[:, i * PP : (i + 1) * PP].astype(bf16)


def conv(meta, field, top, bottom, side, wf, wb, cot):
    return pl.pallas_call(
        conv_kernel,
        grid_spec=pltpu.PrefetchScalarGridSpec(
            num_scalar_prefetch=1,
            grid=(ROWS + 2,),
            in_specs=[
                whole(field.shape),
                whole(top.shape),
                whole(bottom.shape),
                whole(side.shape),
                whole(wf.shape),
                whole(wb.shape),
                pl.BlockSpec((1, HID, WIDE), lambda i, *a: (i, 0, 0)),
            ],
            out_specs=[
                pl.BlockSpec(
                    (1, HID, COLS), lambda i, *a: (jnp.clip(i - 1, 0, ROWS - 1), 0, 0)
                ),
                whole((3, 3 * CP, HID)),
                pl.BlockSpec((4, CP, PP), lambda i, *a: (jnp.maximum(i - 2, 0), 0, 0)),
            ],
            scratch_shapes=[
                pltpu.VMEM((20, 3 * CP, WIDE), bf16),
                pltpu.VMEM((ROWS + 2, HID, WIDE), bf16),
                pltpu.VMEM((HID, WIDE), f32),
            ],
        ),
        out_shape=[
            jax.ShapeDtypeStruct((ROWS, HID, COLS), bf16),
            jax.ShapeDtypeStruct((3, 3 * CP, HID), f32),
            jax.ShapeDtypeStruct((PIECES, CP, PP), bf16),
        ],
        compiler_params=params(),
        name="conv",
    )(meta, field, top, bottom, side, wf, wb, cot)


def reply_kernel(piece_ref, dfield_ref, out_ref):
    step = pl.program_id(0)
    for g in range(GRP):
        parts = []
        for s in range(2):
            piece = piece_ref[(step * GRP + g) * 2 + s]
            parts.append(dfield_ref[piece].astype(f32)[:SL])
        out_ref[g] = jnp.concatenate(parts, axis=0).astype(bf16)


def replies(pieces, dfield):
    return pl.pallas_call(
        reply_kernel,
        grid_spec=pltpu.PrefetchScalarGridSpec(
            num_scalar_prefetch=1,
            grid=(DEVS // GRP,),
            in_specs=[whole(dfield.shape)],
            out_specs=pl.BlockSpec((GRP, 2 * SL, PP), lambda i, *a: (i, 0, 0)),
        ),
        out_shape=jax.ShapeDtypeStruct((DEVS, 2 * SL, PP), bf16),
        compiler_params=params(),
        name="reply",
    )(pieces, dfield)


def final_kernel(place_ref, back_ref, w_ref, out_ref):
    step = pl.program_id(0)
    for g in range(4):
        total = jnp.zeros((SL, PP), f32)
        for j in range(K):
            code = place_ref[(step * 4 + g) * K + j]
            both = back_ref[code >> 2].astype(f32)
            got = jnp.where(((code >> 1) & 1) == 0, both[:SL], both[SL:])
            got = (got * (code & 1).astype(f32)).astype(bf16)
            total += lax.dot_general(
                got, w_ref[g, j], (((1,), (1,)), ((), ())), preferred_element_type=f32
            )
        out_ref[g] = total[:C].astype(bf16)


def final_products(places, back, weight):
    blocks = weight.shape[0]
    return pl.pallas_call(
        final_kernel,
        grid_spec=pltpu.PrefetchScalarGridSpec(
            num_scalar_prefetch=1,
            grid=(blocks // 4,),
            in_specs=[
                whole(back.shape),
                pl.BlockSpec((4, K, PP, PP), lambda i, *a: (i, 0, 0, 0)),
            ],
            out_specs=pl.BlockSpec((4, C, PP), lambda i, *a: (i, 0, 0)),
        ),
        out_shape=jax.ShapeDtypeStruct((blocks, C, PP), bf16),
        compiler_params=params(),
        name="final",
    )(places, back, weight)


def exchange(value):
    return lax.all_to_all(value, ("face", "tile"), split_axis=0, concat_axis=0, tiled=True)


def wide_cotangent(cot):
    up = [(i, i + 1) for i in range(31)]
    down = [(i + 1, i) for i in range(31)]
    cot = jnp.concatenate(
        [
            lax.ppermute(cot[:, ROWS - 1 :], "tile", up),
            cot,
            lax.ppermute(cot[:, :1], "tile", down),
        ],
        axis=1,
    )
    before = lax.ppermute(cot[:, :, COLS - 1 :], "face", [(i, (i + 1) % 4) for i in range(4)])
    after = lax.ppermute(cot[:, :, :1], "face", [((i + 1) % 4, i) for i in range(4)])
    gap = jnp.zeros((HID, ROWS + 2, WIDE - COLS - 2), bf16)
    return jnp.concatenate([cot, after, gap, before], axis=2).transpose(1, 0, 2)


def local(latlon, intersection_weight, target_dev, target_piece, counts, conv_weight, cotangent):
    blocks = latlon.shape[0]
    owners = jnp.arange(DEVS, dtype=jnp.int32)
    live = (jnp.arange(K, dtype=jnp.int32)[None, :] < counts[:, None]).astype(jnp.int32)
    entry = jnp.arange(blocks * K, dtype=jnp.int32).reshape(blocks, K)
    code = (entry * 64 + target_piece) * 2 + live
    mine = target_dev[None] == owners[:, None, None]
    first = jnp.min(jnp.where(mine, code[None], jnp.int32(1 << 24)), axis=(1, 2))
    second = jnp.max(jnp.where(mine, code[None], jnp.int32(-1)), axis=(1, 2))
    keys = jnp.stack([first, second], axis=1).reshape(-1)
    flat = target_dev.reshape(-1)
    order = entry.reshape(-1)
    slot = jnp.sum(
        ((flat[:, None] == flat[None, :]) & (order[None, :] < order[:, None])).astype(jnp.int32),
        axis=1,
    )
    places = flat * 4 + slot * 2 + live.reshape(-1)

    cot = wide_cotangent(cotangent[0])
    send = partial_products(
        keys, latlon, intersection_weight.reshape(blocks * K, PP, PP)
    )
    recv = exchange(send)
    pieces = jnp.stack([recv[:, C, 0], recv[:, SL + C, 0]], axis=1).reshape(-1).astype(jnp.int32)
    field, pack = gather_field(pieces, recv)
    top, bottom, side = halo(field, pack)

    kernel = conv_weight.reshape(3, 3, HID, C)
    kernel = jnp.pad(kernel, ((0, 0), (0, 0), (0, 0), (0, CP - C)))
    wf = kernel.transpose(0, 2, 1, 3).reshape(3, HID, 3 * CP)
    wb = kernel.transpose(0, 1, 3, 2).reshape(3, 3 * CP, HID)
    meta = lax.axis_index("tile").astype(jnp.int32).reshape(1)
    act, grad, dfield = conv(meta, field, top, bottom, side, wf, wb, cot)
    activation = act.transpose(1, 0, 2)[None]

    back = exchange(replies(pieces, dfield))
    shares = exchange(grad.reshape(DEVS, -1))
    share = jnp.sum(shares, axis=0) * (1.0 / math.sqrt(DEVS * ROWS * COLS))
    summed = exchange(jnp.broadcast_to(share[None], (DEVS, share.shape[0])))
    grad_conv = summed.reshape(9, CP, HID)[:, :C].transpose(0, 2, 1)
    grad_latlon = final_products(places, back, intersection_weight)
    return (activation, grad_conv, grad_latlon)


def solution(mesh):
    placed = (
        P(("face", "tile"), None, None),
        P(("face", "tile"), None, None, None),
        P(("face", "tile"), None),
        P(("face", "tile"), None),
        P(("face", "tile")),
        P(),
        P("face", None, "tile", None),
    )
    return jax.shard_map(
        local,
        mesh=mesh,
        in_specs=placed,
        out_specs=(P("face", None, "tile", None), P(), P(("face", "tile"), None, None)),
        check_vma=False,
    )
```

```python
import functools
import math

import jax
import jax.numpy as jnp
from jax import lax
from jax.experimental import pallas as pl
from jax.experimental.pallas import tpu as pltpu
from jax.sharding import PartitionSpec as P

C = 74
CP = 80
SL = 76
HID = 256
ROWS = 16
COLS = 512
WIDE = 640
PP = 128
K = 4
PIECES = 64
DEVS = 128
GRP = 8
SHARE = 11
BACK = 160
VMEM_LIMIT = 63 * 1024 * 1024
MESH = pl.DeviceIdType.MESH
f32 = jnp.float32
bf16 = jnp.bfloat16


def params(**kw):
    return pltpu.CompilerParams(vmem_limit_bytes=VMEM_LIMIT, **kw)


def whole(shape):
    zeros = (0,) * len(shape)
    return pl.BlockSpec(shape, lambda *a: zeros)


def partial_kernel(key_ref, lat_ref, w_ref, out_ref):
    step = pl.program_id(0)
    for g in range(GRP):
        parts = []
        for s in range(2):
            key = key_ref[(step * GRP + g) * 2 + s]
            entry = key >> 7
            alive = (key & 1).astype(f32)
            piece = ((key >> 1) & 63).astype(f32)
            value = jnp.dot(lat_ref[entry >> 2], w_ref[entry], preferred_element_type=f32)
            parts += [value * alive, jnp.full((SL - C, PP), piece, f32)]
        out_ref[g] = jnp.concatenate(parts, axis=0).astype(bf16)


def partial_products(keys, lat, weight):
    return pl.pallas_call(
        partial_kernel,
        grid_spec=pltpu.PrefetchScalarGridSpec(
            num_scalar_prefetch=1,
            grid=(DEVS // GRP,),
            in_specs=[whole(lat.shape), whole(weight.shape)],
            out_specs=pl.BlockSpec((GRP, 2 * SL, PP), lambda i, *a: (i, 0, 0)),
        ),
        out_shape=jax.ShapeDtypeStruct((DEVS, 2 * SL, PP), bf16),
        compiler_params=params(),
        cost_estimate=pl.CostEstimate(
            flops=1_300_000_000, bytes_accessed=15_000_000, transcendentals=0
        ),
        name="partial",
    )(keys, lat, weight)


def gather_kernel(piece_ref, recv_ref, field_ref, pack_ref, acc_ref):
    step = pl.program_id(0)

    @pl.when(step == 0)
    def _():
        acc_ref[...] = jnp.zeros_like(acc_ref)

    for g in range(GRP):
        block = recv_ref[g].astype(f32)
        for s in range(2):
            piece = piece_ref[(step * GRP + g) * 2 + s]
            acc_ref[piece, :SL] += block[s * SL : (s + 1) * SL]

    @pl.when(step == pl.num_programs(0) - 1)
    def _():
        real = lax.broadcasted_iota(jnp.int32, (CP, PP), 0) < C
        lane = lax.broadcasted_iota(jnp.int32, (CP, PP), 1)
        left = jnp.zeros((CP, PP), f32)
        right = jnp.zeros((CP, PP), f32)
        for r in range(ROWS):
            for i in range(4):
                tile = jnp.where(real, acc_ref[r * 4 + i], 0.0)
                field_ref[r * 4 + i] = tile.astype(bf16)
                mine = (lane >> 1) == r
                if i == 0:
                    left = jnp.where(mine, pltpu.roll(tile, 2 * r, 1) if r else tile, left)
                if i == 3:
                    right = jnp.where(mine, pltpu.roll(tile, 2 * r + 2, 1), right)
        pack_ref[0] = left.astype(bf16)
        pack_ref[1] = right.astype(bf16)


def gather_field(pieces, recv):
    return pl.pallas_call(
        gather_kernel,
        grid_spec=pltpu.PrefetchScalarGridSpec(
            num_scalar_prefetch=1,
            grid=(DEVS // GRP,),
            in_specs=[pl.BlockSpec((GRP, 2 * SL, PP), lambda i, *a: (i, 0, 0))],
            out_specs=[whole((PIECES, CP, PP)), whole((2, CP, PP))],
            scratch_shapes=[pltpu.VMEM((PIECES, CP, PP), f32)],
        ),
        out_shape=[
            jax.ShapeDtypeStruct((PIECES, CP, PP), bf16),
            jax.ShapeDtypeStruct((2, CP, PP), bf16),
        ],
        compiler_params=params(),
        name="gather_field",
    )(pieces, recv)


def halo_kernel(field_ref, pack_ref, top_ref, bottom_ref, side_ref, send_sem, recv_sem):
    face = lax.axis_index("face")
    tile = lax.axis_index("tile")

    def at(df, dt):
        return (lax.rem(face + df + 4, 4), lax.rem(tile + dt + 32, 32))

    plan = [
        (field_ref.at[pl.ds(56, 8)], top_ref, at(0, 1)),
        (field_ref.at[pl.ds(0, 8)], bottom_ref, at(0, -1)),
    ]
    for dt in (-1, 0, 1):
        plan.append((pack_ref.at[1], side_ref.at[1 - dt], at(1, dt)))
        plan.append((pack_ref.at[0], side_ref.at[4 - dt], at(-1, dt)))
    barrier = pltpu.get_barrier_semaphore()
    for _, _, to in plan:
        pl.semaphore_signal(barrier, inc=1, device_id=to, device_id_type=MESH)
    pl.semaphore_wait(barrier, len(plan))
    copies = [
        pltpu.make_async_remote_copy(
            src_ref=src,
            dst_ref=dst,
            send_sem=send_sem.at[i],
            recv_sem=recv_sem.at[i],
            device_id=to,
            device_id_type=MESH,
        )
        for i, (src, dst, to) in enumerate(plan)
    ]
    for copy in copies:
        copy.start()
    for copy in copies:
        copy.wait()


def halo(field, pack):
    vmem = pl.BlockSpec(memory_space=pltpu.VMEM)
    return pl.pallas_call(
        halo_kernel,
        in_specs=[vmem, vmem],
        out_specs=[vmem, vmem, vmem],
        out_shape=[
            jax.ShapeDtypeStruct((8, CP, PP), bf16),
            jax.ShapeDtypeStruct((8, CP, PP), bf16),
            jax.ShapeDtypeStruct((6, CP, PP), bf16),
        ],
        scratch_shapes=[pltpu.SemaphoreType.DMA((8,)), pltpu.SemaphoreType.DMA((8,))],
        compiler_params=pltpu.CompilerParams(collective_id=0, has_side_effects=True),
        name="halo",
    )(field, pack)


def conv_kernel(
    meta_ref, field_ref, top_ref, bottom_ref, side_ref, wf_ref, wb_ref, cot_ref, rim_ref, edge_ref,
    act_ref, rows_ref, dfield_ref, x_ref, d_ref, pre_ref, grad_ref,
):
    step = pl.program_id(0)

    @pl.when(step == 0)
    def _():
        tile_at = meta_ref[0]
        has_top = (tile_at != 0).astype(f32)
        has_bottom = (tile_at != 31).astype(f32)
        lane = lax.broadcasted_iota(jnp.int32, (CP, PP), 1)

        def row(q, tiles, lefts, rights, at, factor):
            ext_l = pltpu.roll(lefts, (254 - 2 * at) % 128, 1) if 2 * at != 126 else lefts
            ext_r = pltpu.roll(rights, (128 - 2 * at) % 128, 1) if at else rights
            ext = jnp.where(lane < 2, ext_r, jnp.where(lane >= 126, ext_l, 0.0))
            full = jnp.concatenate(tiles + [ext], axis=1)
            if factor is not None:
                full = full * factor
            x_ref[q, 0:CP] = pltpu.roll(full, 1, 1).astype(bf16)
            x_ref[q, CP : 2 * CP] = full.astype(bf16)
            x_ref[q, 2 * CP : 3 * CP] = pltpu.roll(full, WIDE - 1, 1).astype(bf16)

        sides = [side_ref[i].astype(f32) for i in range(6)]
        for q in range(20):
            if q < 2:
                tiles = [top_ref[q * 4 + i].astype(f32) for i in range(4)]
                row(q, tiles, sides[0], sides[3], 14 + q, has_top)
            elif q < 18:
                tiles = [field_ref[(q - 2) * 4 + i].astype(f32) for i in range(4)]
                row(q, tiles, sides[1], sides[4], q - 2, None)
            else:
                tiles = [bottom_ref[(q - 18) * 4 + i].astype(f32) for i in range(4)]
                row(q, tiles, sides[2], sides[5], q - 18, has_bottom)
        grad_ref[...] = jnp.zeros_like(grad_ref)

    total = jnp.dot(wf_ref[0], x_ref[step], preferred_element_type=f32)
    total += jnp.dot(wf_ref[1], x_ref[step + 1], preferred_element_type=f32)
    total += jnp.dot(wf_ref[2], x_ref[step + 2], preferred_element_type=f32)
    pre_ref[...] = total
    for at in range(0, HID, 32):
        v = pre_ref[at : at + 32]
        square = v * v
        t = jnp.tanh(v * (0.7978845608 + (0.7978845608 * 0.044715) * square))
        half = 0.5 + 0.5 * t
        result = v * half
        slope = half + result * (1.0 - t) * (0.7978845608 + (0.7978845608 * 0.134145) * square)

        @pl.when((step >= 1) & (step <= ROWS))
        def _():
            act_ref[0, at : at + 32] = result[:, :COLS].astype(bf16)

        inner = (step >= 1) & (step <= ROWS)
        cot = jnp.where(inner, cot_ref[0, at : at + 32], rim_ref[0, at : at + 32]).astype(f32)
        edge = edge_ref[0, at : at + 32].astype(f32)
        d_ref[step, at : at + 32, :COLS] = (cot * slope[:, :COLS]).astype(bf16)
        d_ref[step, at : at + 32, COLS:] = (edge * slope[:, COLS:]).astype(bf16)

    @pl.when((step >= 1) & (step <= ROWS))
    def _():
        dpre = d_ref[step][:, :COLS]
        for ky in range(3):
            grad_ref[ky] += lax.dot_general(
                x_ref[step + ky][:, :COLS], dpre, (((1,), (1,)), ((), ())),
                preferred_element_type=f32,
            )

    @pl.when(step >= 2)
    def _():
        back = jnp.dot(wb_ref[0], d_ref[step], preferred_element_type=f32)
        back += jnp.dot(wb_ref[1], d_ref[step - 1], preferred_element_type=f32)
        back += jnp.dot(wb_ref[2], d_ref[step - 2], preferred_element_type=f32)
        out = (
            pltpu.roll(back[0:CP], WIDE - 1, 1)
            + back[CP : 2 * CP]
            + pltpu.roll(back[2 * CP : 3 * CP], 1, 1)
        )
        for i in range(4):
            dfield_ref[i] = out[:, i * PP : (i + 1) * PP].astype(bf16)

    @pl.when(step == pl.num_programs(0) - 1)
    def _():
        for h in range(2):
            for k in range(9):
                at = (k % 3) * CP
                rows_ref[pl.ds((h * 9 + k) * C, C)] = grad_ref[
                    k // 3, at : at + C, h * PP : (h + 1) * PP
                ]
        rows_ref[pl.ds(18 * C, DEVS * SHARE - 18 * C)] = jnp.zeros(
            (DEVS * SHARE - 18 * C, PP), f32
        )


def conv(meta, field, top, bottom, side, wf, wb, cots):
    return pl.pallas_call(
        conv_kernel,
        grid_spec=pltpu.PrefetchScalarGridSpec(
            num_scalar_prefetch=1,
            grid=(ROWS + 2,),
            in_specs=[
                whole(field.shape),
                whole(top.shape),
                whole(bottom.shape),
                whole(side.shape),
                whole(wf.shape),
                whole(wb.shape),
                pl.BlockSpec(
                    (1, HID, COLS), lambda i, *a: (jnp.clip(i - 1, 0, ROWS - 1), 0, 0)
                ),
                pl.BlockSpec((1, HID, COLS), lambda i, *a: (jnp.minimum(i, 1), 0, 0)),
                pl.BlockSpec((1, HID, PP), lambda i, *a: (i, 0, 0)),
            ],
            out_specs=[
                pl.BlockSpec(
                    (1, HID, COLS), lambda i, *a: (jnp.clip(i - 1, 0, ROWS - 1), 0, 0)
                ),
                whole((DEVS * SHARE, PP)),
                pl.BlockSpec((4, CP, PP), lambda i, *a: (jnp.maximum(i - 2, 0), 0, 0)),
            ],
            scratch_shapes=[
                pltpu.VMEM((20, 3 * CP, WIDE), bf16),
                pltpu.VMEM((ROWS + 2, HID, WIDE), bf16),
                pltpu.VMEM((HID, WIDE), f32),
                pltpu.VMEM((3, 3 * CP, HID), f32),
            ],
        ),
        out_shape=[
            jax.ShapeDtypeStruct((ROWS, HID, COLS), bf16),
            jax.ShapeDtypeStruct((DEVS * SHARE, PP), f32),
            jax.ShapeDtypeStruct((PIECES, CP, PP), bf16),
        ],
        compiler_params=params(),
        name="conv",
    )(meta, field, top, bottom, side, wf, wb, *cots)


def channel_major_kernel(in_ref, out_ref, turn_ref):
    for i in range(COLS // PP):
        for r in range(ROWS):
            turn_ref[i, pl.ds(r, 32, stride=ROWS), :] = in_ref[
                r, :, i * PP : (i + 1) * PP
            ].astype(f32)
    for i in range(COLS // PP):
        for o in range(32):
            out_ref[o, :, i * PP : (i + 1) * PP] = turn_ref[
                i, o * ROWS : (o + 1) * ROWS
            ].astype(bf16)


def channel_major(act):
    return pl.pallas_call(
        channel_major_kernel,
        grid=(HID // 32,),
        in_specs=[pl.BlockSpec((ROWS, 32, COLS), lambda i: (0, i, 0))],
        out_specs=pl.BlockSpec((32, ROWS, COLS), lambda i: (i, 0, 0)),
        out_shape=jax.ShapeDtypeStruct((HID, ROWS, COLS), bf16),
        scratch_shapes=[pltpu.VMEM((COLS // PP, 32 * ROWS, PP), f32)],
        compiler_params=params(),
        cost_estimate=pl.CostEstimate(
            flops=20_000_000, bytes_accessed=160_000_000, transcendentals=0
        ),
        name="channel_major",
    )(act)


def reply_kernel(piece_ref, dfield_ref, rows_ref, out_ref):
    step = pl.program_id(0)
    terms = rows_ref[...]
    for g in range(GRP):
        parts = []
        for s in range(2):
            piece = piece_ref[(step * GRP + g) * 2 + s]
            parts.append(dfield_ref[piece].astype(f32)[:C])
        parts.append(terms[g * SHARE : (g + 1) * SHARE])
        parts.append(jnp.zeros((BACK - 2 * C - SHARE, PP), f32))
        out_ref[g] = jnp.concatenate(parts, axis=0).astype(bf16)


def replies(pieces, dfield, rows):
    return pl.pallas_call(
        reply_kernel,
        grid_spec=pltpu.PrefetchScalarGridSpec(
            num_scalar_prefetch=1,
            grid=(DEVS // GRP,),
            in_specs=[
                whole(dfield.shape),
                pl.BlockSpec((GRP * SHARE, PP), lambda i, *a: (i, 0)),
            ],
            out_specs=pl.BlockSpec((GRP, BACK, PP), lambda i, *a: (i, 0, 0)),
        ),
        out_shape=jax.ShapeDtypeStruct((DEVS, BACK, PP), bf16),
        compiler_params=params(),
        name="reply",
    )(pieces, dfield, rows)


def final_kernel(place_ref, back_hbm, w_ref, out_ref, back_ref, sem):
    step = pl.program_id(0)

    @pl.when(step == 0)
    def _():
        copy = pltpu.make_async_copy(back_hbm, back_ref, sem)
        copy.start()
        copy.wait()

    for g in range(4):
        total = jnp.zeros((C, PP), f32)
        for j in range(K):
            code = place_ref[(step * 4 + g) * K + j]
            both = back_ref[code >> 2].astype(f32)
            got = jnp.where(((code >> 1) & 1) == 0, both[:C], both[C : 2 * C])
            got = (got * (code & 1).astype(f32)).astype(bf16)
            total += lax.dot_general(
                got, w_ref[g, j], (((1,), (1,)), ((), ())), preferred_element_type=f32
            )
        out_ref[g] = total.astype(bf16)


def final_products(places, back, weight):
    blocks = weight.shape[0]
    return pl.pallas_call(
        final_kernel,
        grid_spec=pltpu.PrefetchScalarGridSpec(
            num_scalar_prefetch=1,
            grid=(blocks // 4,),
            in_specs=[
                pl.BlockSpec(memory_space=pltpu.HBM),
                pl.BlockSpec((4, K, PP, PP), lambda i, *a: (i, 0, 0, 0)),
            ],
            out_specs=pl.BlockSpec((4, C, PP), lambda i, *a: (i, 0, 0)),
            scratch_shapes=[pltpu.VMEM(back.shape, bf16), pltpu.SemaphoreType.DMA],
        ),
        out_shape=jax.ShapeDtypeStruct((blocks, C, PP), bf16),
        compiler_params=params(),
        cost_estimate=pl.CostEstimate(
            flops=1_300_000_000, bytes_accessed=30_000_000, transcendentals=0
        ),
        name="final",
    )(places, back, weight)


def exchange(value):
    return lax.all_to_all(value, ("face", "tile"), split_axis=0, concat_axis=0, tiled=True)


def cotangent_rim(cot):
    up = [(i, i + 1) for i in range(31)]
    down = [(i + 1, i) for i in range(31)]
    above = lax.ppermute(cot[:, ROWS - 1 :], "tile", up)
    below = lax.ppermute(cot[:, :1], "tile", down)
    ends = jnp.concatenate([above, cot, below], axis=1)
    last, first = ends[:, :, COLS - 1 :], ends[:, :, :1]
    before = lax.ppermute(last, "face", [(i, (i + 1) % 4) for i in range(4)])
    after = lax.ppermute(first, "face", [((i + 1) % 4, i) for i in range(4)])
    gap = jnp.zeros((HID, ROWS + 2, PP - 2), bf16)
    side = jnp.concatenate([after, gap, before], axis=2).transpose(1, 0, 2)
    rim = jnp.concatenate([above, below], axis=1).transpose(1, 0, 2)
    return cot.transpose(1, 0, 2), rim, side


def local(latlon, intersection_weight, target_dev, target_piece, counts, conv_weight, cotangent):
    blocks = latlon.shape[0]
    owners = jnp.arange(DEVS, dtype=jnp.int32)
    live = (jnp.arange(K, dtype=jnp.int32)[None, :] < counts[:, None]).astype(jnp.int32)
    entry = jnp.arange(blocks * K, dtype=jnp.int32).reshape(blocks, K)
    code = (entry * 64 + target_piece) * 2 + live
    mine = target_dev[None] == owners[:, None, None]
    first = jnp.min(jnp.where(mine, code[None], jnp.int32(1 << 24)), axis=(1, 2))
    second = jnp.max(jnp.where(mine, code[None], jnp.int32(-1)), axis=(1, 2))
    keys = jnp.stack([first, second], axis=1).reshape(-1)
    flat = target_dev.reshape(-1)
    order = entry.reshape(-1)
    slot = jnp.sum(
        ((flat[:, None] == flat[None, :]) & (order[None, :] < order[:, None])).astype(jnp.int32),
        axis=1,
    )
    places = flat * 4 + slot * 2 + live.reshape(-1)

    cots = cotangent_rim(cotangent[0])
    send = partial_products(
        keys, latlon, intersection_weight.reshape(blocks * K, PP, PP)
    )
    recv = exchange(send)
    pieces = jnp.stack([recv[:, C, 0], recv[:, SL + C, 0]], axis=1).reshape(-1).astype(jnp.int32)
    field, pack = gather_field(pieces, recv)
    top, bottom, side = halo(field, pack)

    kernel = conv_weight.reshape(3, 3, HID, C)
    kernel = jnp.pad(kernel, ((0, 0), (0, 0), (0, 0), (0, CP - C)))
    wf = kernel.transpose(0, 2, 1, 3).reshape(3, HID, 3 * CP)
    wb = kernel.transpose(0, 1, 3, 2).reshape(3, 3 * CP, HID)
    meta = lax.axis_index("tile").astype(jnp.int32).reshape(1)
    act, rows, dfield = conv(meta, field, top, bottom, side, wf, wb, cots)
    activation = channel_major(act)[None]

    back = exchange(replies(pieces, dfield, rows))
    share = jnp.sum(back[:, 2 * C : 2 * C + SHARE].astype(f32), axis=0)
    share = (share * (1.0 / math.sqrt(DEVS * ROWS * COLS))).astype(bf16)
    summed = exchange(jnp.broadcast_to(share[None], (DEVS, SHARE, PP)))
    summed = summed.reshape(DEVS * SHARE, PP)[: 18 * C].reshape(2, 9, C, PP)
    grad_conv = summed.astype(f32).transpose(1, 0, 3, 2).reshape(9, HID, C)
    grad_latlon = final_products(places, back, intersection_weight)
    return (activation, grad_conv, grad_latlon)


def solution(mesh):
    placed = (
        P(("face", "tile"), None, None),
        P(("face", "tile"), None, None, None),
        P(("face", "tile"), None),
        P(("face", "tile"), None),
        P(("face", "tile")),
        P(),
        P("face", None, "tile", None),
    )
    return jax.shard_map(
        local,
        mesh=mesh,
        in_specs=placed,
        out_specs=(P("face", None, "tile", None), P(), P(("face", "tile"), None, None)),
        check_vma=False,
    )
```

```python
import math

import jax
import jax.numpy as jnp
from jax import lax
from jax.experimental import pallas as pl
from jax.experimental.pallas import tpu as pltpu
from jax.sharding import PartitionSpec as P


C = 74
CP = 80
SL = 76
HID = 256
ROWS = 16
COLS = 512
WIDE = 640
PP = 128
K = 4
PIECES = 64
DEVS = 128
GRP = 32
SUB = 8
SHARE = 11
BACK = 160
VMEM_LIMIT = 63 * 1024 * 1024
MESH = pl.DeviceIdType.MESH
f32 = jnp.float32
bf16 = jnp.bfloat16


def params(**kw):
    return pltpu.CompilerParams(vmem_limit_bytes=VMEM_LIMIT, **kw)


def whole(shape):
    zeros = (0,) * len(shape)
    return pl.BlockSpec(shape, lambda *a: zeros)


def partial_kernel(key_ref, lat_ref, w_ref, out_ref, rows_ref):
    step = pl.program_id(0)
    blocks = lat_ref.shape[1]

    @pl.when(step == 0)
    def _():
        for c in range(C):
            rows_ref[c * blocks : (c + 1) * blocks] = lat_ref[c].astype(f32)

    def body(i, carry):
        for g in range(SUB):
            parts = []
            for s in range(2):
                key = key_ref[(step * GRP + i * SUB + g) * 2 + s]
                entry = key >> 7
                alive = (key & 1).astype(f32)
                piece = ((key >> 1) & 63).astype(f32)
                lat = rows_ref[pl.ds(entry >> 2, C, stride=blocks), :].astype(bf16)
                value = jnp.dot(lat, w_ref[entry], preferred_element_type=f32)
                parts += [value * alive, jnp.full((SL - C, PP), piece, f32)]
            out_ref[i * SUB + g] = jnp.concatenate(parts, axis=0).astype(bf16)
        return carry

    lax.fori_loop(0, GRP // SUB, body, 0)


def partial_products(keys, lat, weight):
    return pl.pallas_call(
        partial_kernel,
        grid_spec=pltpu.PrefetchScalarGridSpec(
            num_scalar_prefetch=1,
            grid=(DEVS // GRP,),
            in_specs=[whole(lat.shape), whole(weight.shape)],
            out_specs=pl.BlockSpec((GRP, 2 * SL, PP), lambda i, *a: (i, 0, 0)),
            scratch_shapes=[pltpu.VMEM((C * lat.shape[1], PP), f32)],
        ),
        out_shape=jax.ShapeDtypeStruct((DEVS, 2 * SL, PP), bf16),
        compiler_params=params(),
        cost_estimate=pl.CostEstimate(
            flops=1_300_000_000, bytes_accessed=15_000_000, transcendentals=0
        ),
        name="partial",
    )(keys, lat, weight)


def gather_kernel(piece_ref, recv_ref, field_ref, pack_ref, acc_ref):
    step = pl.program_id(0)

    @pl.when(step == 0)
    def _():
        acc_ref[...] = jnp.zeros_like(acc_ref)

    def body(i, carry):
        for g in range(SUB):
            block = recv_ref[i * SUB + g].astype(f32)
            for s in range(2):
                piece = piece_ref[(step * GRP + i * SUB + g) * 2 + s]
                acc_ref[piece, :SL] += block[s * SL : (s + 1) * SL]
        return carry

    lax.fori_loop(0, GRP // SUB, body, 0)

    @pl.when(step == pl.num_programs(0) - 1)
    def _():
        real = lax.broadcasted_iota(jnp.int32, (CP, PP), 0) < C
        lane = lax.broadcasted_iota(jnp.int32, (CP, PP), 1)
        left = jnp.zeros((CP, PP), f32)
        right = jnp.zeros((CP, PP), f32)
        for r in range(ROWS):
            for i in range(4):
                tile = jnp.where(real, acc_ref[r * 4 + i], 0.0)
                field_ref[r * 4 + i] = tile.astype(bf16)
                mine = (lane >> 1) == r
                if i == 0:
                    left = jnp.where(mine, pltpu.roll(tile, 2 * r, 1) if r else tile, left)
                if i == 3:
                    right = jnp.where(mine, pltpu.roll(tile, 2 * r + 2, 1), right)
        pack_ref[0] = left.astype(bf16)
        pack_ref[1] = right.astype(bf16)


def gather_field(pieces, recv):
    return pl.pallas_call(
        gather_kernel,
        grid_spec=pltpu.PrefetchScalarGridSpec(
            num_scalar_prefetch=1,
            grid=(DEVS // GRP,),
            in_specs=[pl.BlockSpec((GRP, 2 * SL, PP), lambda i, *a: (i, 0, 0))],
            out_specs=[whole((PIECES, CP, PP)), whole((2, CP, PP))],
            scratch_shapes=[pltpu.VMEM((PIECES, CP, PP), f32)],
        ),
        out_shape=[
            jax.ShapeDtypeStruct((PIECES, CP, PP), bf16),
            jax.ShapeDtypeStruct((2, CP, PP), bf16),
        ],
        compiler_params=params(),
        name="gather_field",
    )(pieces, recv)


def halo_kernel(field_ref, pack_ref, top_ref, bottom_ref, side_ref, send_sem, recv_sem):
    face = lax.axis_index("face")
    tile = lax.axis_index("tile")

    def at(df, dt):
        return (lax.rem(face + df + 4, 4), lax.rem(tile + dt + 32, 32))

    plan = [
        (field_ref.at[pl.ds(56, 8)], top_ref, at(0, 1)),
        (field_ref.at[pl.ds(0, 8)], bottom_ref, at(0, -1)),
    ]
    for dt in (-1, 0, 1):
        plan.append((pack_ref.at[1], side_ref.at[1 - dt], at(1, dt)))
        plan.append((pack_ref.at[0], side_ref.at[4 - dt], at(-1, dt)))
    barrier = pltpu.get_barrier_semaphore()
    for _, _, to in plan:
        pl.semaphore_signal(barrier, inc=1, device_id=to, device_id_type=MESH)
    pl.semaphore_wait(barrier, len(plan))
    copies = [
        pltpu.make_async_remote_copy(
            src_ref=src,
            dst_ref=dst,
            send_sem=send_sem.at[i],
            recv_sem=recv_sem.at[i],
            device_id=to,
            device_id_type=MESH,
        )
        for i, (src, dst, to) in enumerate(plan)
    ]
    for copy in copies:
        copy.start()
    for copy in copies:
        copy.wait()


def halo(field, pack):
    vmem = pl.BlockSpec(memory_space=pltpu.VMEM)
    return pl.pallas_call(
        halo_kernel,
        in_specs=[vmem, vmem],
        out_specs=[vmem, vmem, vmem],
        out_shape=[
            jax.ShapeDtypeStruct((8, CP, PP), bf16),
            jax.ShapeDtypeStruct((8, CP, PP), bf16),
            jax.ShapeDtypeStruct((6, CP, PP), bf16),
        ],
        scratch_shapes=[pltpu.SemaphoreType.DMA((8,)), pltpu.SemaphoreType.DMA((8,))],
        compiler_params=pltpu.CompilerParams(collective_id=0, has_side_effects=True),
        name="halo",
    )(field, pack)


def conv_kernel(
    meta_ref, field_ref, top_ref, bottom_ref, side_ref, wf_ref, wb_ref, cot_ref, rim_ref, edge_ref,
    act_ref, rows_ref, dfield_ref, x_ref, d_ref, pre_ref, grad_ref,
):
    step = pl.program_id(0)

    @pl.when(step == 0)
    def _():
        tile_at = meta_ref[0]
        has_top = (tile_at != 0).astype(f32)
        has_bottom = (tile_at != 31).astype(f32)
        lane = lax.broadcasted_iota(jnp.int32, (CP, PP), 1)

        def row(q, tiles, lefts, rights, at, factor):
            ext_l = pltpu.roll(lefts, (254 - 2 * at) % 128, 1) if 2 * at != 126 else lefts
            ext_r = pltpu.roll(rights, (128 - 2 * at) % 128, 1) if at else rights
            ext = jnp.where(lane < 2, ext_r, jnp.where(lane >= 126, ext_l, 0.0))
            full = jnp.concatenate(tiles + [ext], axis=1)
            if factor is not None:
                full = full * factor
            x_ref[q, 0:CP] = pltpu.roll(full, 1, 1).astype(bf16)
            x_ref[q, CP : 2 * CP] = full.astype(bf16)
            x_ref[q, 2 * CP : 3 * CP] = pltpu.roll(full, WIDE - 1, 1).astype(bf16)

        sides = [side_ref[i].astype(f32) for i in range(6)]
        for q in range(20):
            if q < 2:
                tiles = [top_ref[q * 4 + i].astype(f32) for i in range(4)]
                row(q, tiles, sides[0], sides[3], 14 + q, has_top)
            elif q < 18:
                tiles = [field_ref[(q - 2) * 4 + i].astype(f32) for i in range(4)]
                row(q, tiles, sides[1], sides[4], q - 2, None)
            else:
                tiles = [bottom_ref[(q - 18) * 4 + i].astype(f32) for i in range(4)]
                row(q, tiles, sides[2], sides[5], q - 18, has_bottom)
        grad_ref[...] = jnp.zeros_like(grad_ref)

    total = jnp.dot(wf_ref[0], x_ref[step], preferred_element_type=f32)
    total += jnp.dot(wf_ref[1], x_ref[step + 1], preferred_element_type=f32)
    total += jnp.dot(wf_ref[2], x_ref[step + 2], preferred_element_type=f32)
    pre_ref[...] = total
    for at in range(0, HID, 32):
        v = pre_ref[at : at + 32]
        square = v * v
        t = jnp.tanh(v * (0.7978845608 + (0.7978845608 * 0.044715) * square))
        half = 0.5 + 0.5 * t
        result = v * half
        slope = half + result * (1.0 - t) * (0.7978845608 + (0.7978845608 * 0.134145) * square)

        @pl.when((step >= 1) & (step <= ROWS))
        def _():
            act_ref[0, at : at + 32] = result[:, :COLS].astype(bf16)

        inner = (step >= 1) & (step <= ROWS)
        cot = jnp.where(inner, cot_ref[0, at : at + 32], rim_ref[0, at : at + 32]).astype(f32)
        edge = edge_ref[0, at : at + 32].astype(f32)
        d_ref[step, at : at + 32, :COLS] = (cot * slope[:, :COLS]).astype(bf16)
        d_ref[step, at : at + 32, COLS:] = (edge * slope[:, COLS:]).astype(bf16)

    @pl.when((step >= 1) & (step <= ROWS))
    def _():
        dpre = d_ref[step][:, :COLS]
        for ky in range(3):
            grad_ref[ky] += lax.dot_general(
                x_ref[step + ky][:, :COLS], dpre, (((1,), (1,)), ((), ())),
                preferred_element_type=f32,
            )

    @pl.when(step >= 2)
    def _():
        back = jnp.dot(wb_ref[0], d_ref[step], preferred_element_type=f32)
        back += jnp.dot(wb_ref[1], d_ref[step - 1], preferred_element_type=f32)
        back += jnp.dot(wb_ref[2], d_ref[step - 2], preferred_element_type=f32)
        out = (
            pltpu.roll(back[0:CP], WIDE - 1, 1)
            + back[CP : 2 * CP]
            + pltpu.roll(back[2 * CP : 3 * CP], 1, 1)
        )
        for i in range(4):
            dfield_ref[i] = out[:, i * PP : (i + 1) * PP].astype(bf16)

    @pl.when(step == pl.num_programs(0) - 1)
    def _():
        for h in range(2):
            for k in range(9):
                at = (k % 3) * CP
                rows_ref[pl.ds((h * 9 + k) * C, C)] = grad_ref[
                    k // 3, at : at + C, h * PP : (h + 1) * PP
                ]
        rows_ref[pl.ds(18 * C, DEVS * SHARE - 18 * C)] = jnp.zeros(
            (DEVS * SHARE - 18 * C, PP), f32
        )


def conv(meta, field, top, bottom, side, wf, wb, cots):
    return pl.pallas_call(
        conv_kernel,
        grid_spec=pltpu.PrefetchScalarGridSpec(
            num_scalar_prefetch=1,
            grid=(ROWS + 2,),
            in_specs=[
                whole(field.shape),
                whole(top.shape),
                whole(bottom.shape),
                whole(side.shape),
                whole(wf.shape),
                whole(wb.shape),
                pl.BlockSpec(
                    (1, HID, COLS), lambda i, *a: (jnp.clip(i - 1, 0, ROWS - 1), 0, 0)
                ),
                pl.BlockSpec((1, HID, COLS), lambda i, *a: (jnp.minimum(i, 1), 0, 0)),
                pl.BlockSpec((1, HID, PP), lambda i, *a: (i, 0, 0)),
            ],
            out_specs=[
                pl.BlockSpec(
                    (1, HID, COLS), lambda i, *a: (jnp.clip(i - 1, 0, ROWS - 1), 0, 0)
                ),
                whole((DEVS * SHARE, PP)),
                pl.BlockSpec((4, CP, PP), lambda i, *a: (jnp.maximum(i - 2, 0), 0, 0)),
            ],
            scratch_shapes=[
                pltpu.VMEM((20, 3 * CP, WIDE), bf16),
                pltpu.VMEM((ROWS + 2, HID, WIDE), bf16),
                pltpu.VMEM((HID, WIDE), f32),
                pltpu.VMEM((3, 3 * CP, HID), f32),
            ],
        ),
        out_shape=[
            jax.ShapeDtypeStruct((ROWS, HID, COLS), bf16),
            jax.ShapeDtypeStruct((DEVS * SHARE, PP), f32),
            jax.ShapeDtypeStruct((PIECES, CP, PP), bf16),
        ],
        compiler_params=params(),
        name="conv",
    )(meta, field, top, bottom, side, wf, wb, *cots)


def channel_major_kernel(in_ref, out_ref, turn_ref):
    for i in range(COLS // PP):
        for r in range(ROWS):
            turn_ref[i, pl.ds(r, 32, stride=ROWS), :] = in_ref[
                r, :, i * PP : (i + 1) * PP
            ].astype(f32)
    for i in range(COLS // PP):
        for o in range(32):
            out_ref[o, :, i * PP : (i + 1) * PP] = turn_ref[
                i, o * ROWS : (o + 1) * ROWS
            ].astype(bf16)


def channel_major(act):
    return pl.pallas_call(
        channel_major_kernel,
        grid=(HID // 32,),
        in_specs=[pl.BlockSpec((ROWS, 32, COLS), lambda i: (0, i, 0))],
        out_specs=pl.BlockSpec((32, ROWS, COLS), lambda i: (i, 0, 0)),
        out_shape=jax.ShapeDtypeStruct((HID, ROWS, COLS), bf16),
        scratch_shapes=[pltpu.VMEM((COLS // PP, 32 * ROWS, PP), f32)],
        compiler_params=params(),
        cost_estimate=pl.CostEstimate(
            flops=20_000_000, bytes_accessed=160_000_000, transcendentals=0
        ),
        name="channel_major",
    )(act)


def reply_kernel(piece_ref, dfield_ref, rows_ref, out_ref):
    step = pl.program_id(0)

    def body(i, carry):
        terms = rows_ref[pl.ds(pl.multiple_of(i * (SUB * SHARE), 8), SUB * SHARE)]
        for g in range(SUB):
            parts = []
            for s in range(2):
                piece = piece_ref[(step * GRP + i * SUB + g) * 2 + s]
                parts.append(dfield_ref[piece].astype(f32)[:C])
            parts.append(terms[g * SHARE : (g + 1) * SHARE])
            parts.append(jnp.zeros((BACK - 2 * C - SHARE, PP), f32))
            out_ref[i * SUB + g] = jnp.concatenate(parts, axis=0).astype(bf16)
        return carry

    lax.fori_loop(0, GRP // SUB, body, 0)


def replies(pieces, dfield, rows):
    return pl.pallas_call(
        reply_kernel,
        grid_spec=pltpu.PrefetchScalarGridSpec(
            num_scalar_prefetch=1,
            grid=(DEVS // GRP,),
            in_specs=[
                whole(dfield.shape),
                pl.BlockSpec((GRP * SHARE, PP), lambda i, *a: (i, 0)),
            ],
            out_specs=pl.BlockSpec((GRP, BACK, PP), lambda i, *a: (i, 0, 0)),
        ),
        out_shape=jax.ShapeDtypeStruct((DEVS, BACK, PP), bf16),
        compiler_params=params(),
        name="reply",
    )(pieces, dfield, rows)


def final_kernel(place_ref, back_hbm, w_ref, out_ref, back_ref, rows_ref, sem):
    step = pl.program_id(0)
    blocks = out_ref.shape[1]
    part = DEVS // 4

    @pl.when(step == 0)
    def _():
        copies = [
            pltpu.make_async_copy(
                back_hbm.at[pl.ds(i * part, part)], back_ref.at[pl.ds(i * part, part)], sem.at[i]
            )
            for i in range(4)
        ]
        for copy in copies:
            copy.start()
        for copy in copies:
            copy.wait()

    def body(i, carry):
        for g in range(4):
            here = i * 4 + g
            total = jnp.zeros((C, PP), f32)
            for j in range(K):
                code = place_ref[(step * 16 + here) * K + j]
                both = back_ref[code >> 2].astype(f32)
                got = jnp.where(((code >> 1) & 1) == 0, both[:C], both[C : 2 * C])
                got = (got * (code & 1).astype(f32)).astype(bf16)
                total += lax.dot_general(
                    got, w_ref[here, j], (((1,), (1,)), ((), ())), preferred_element_type=f32
                )
            rows_ref[pl.ds(step * 16 + here, C, stride=blocks), :] = total
        return carry

    lax.fori_loop(0, 4, body, 0)

    @pl.when(step == pl.num_programs(0) - 1)
    def _():
        for c in range(C):
            out_ref[c] = rows_ref[c * blocks : (c + 1) * blocks].astype(bf16)


def final_products(places, back, weight):
    blocks = weight.shape[0]
    return pl.pallas_call(
        final_kernel,
        grid_spec=pltpu.PrefetchScalarGridSpec(
            num_scalar_prefetch=1,
            grid=(blocks // 16,),
            in_specs=[
                pl.BlockSpec(memory_space=pltpu.HBM),
                pl.BlockSpec((16, K, PP, PP), lambda i, *a: (i, 0, 0, 0)),
            ],
            out_specs=whole((C, blocks, PP)),
            scratch_shapes=[
                pltpu.VMEM(back.shape, bf16),
                pltpu.VMEM((C * blocks, PP), f32),
                pltpu.SemaphoreType.DMA((4,)),
            ],
        ),
        out_shape=jax.ShapeDtypeStruct((C, blocks, PP), bf16),
        compiler_params=params(),
        cost_estimate=pl.CostEstimate(
            flops=1_300_000_000, bytes_accessed=30_000_000, transcendentals=0
        ),
        name="final",
    )(places, back, weight)


def exchange(value):
    return lax.all_to_all(value, ("face", "tile"), split_axis=0, concat_axis=0, tiled=True)


def cotangent_rim(cot):
    up = [(i, i + 1) for i in range(31)]
    down = [(i + 1, i) for i in range(31)]
    above = lax.ppermute(cot[:, ROWS - 1 :], "tile", up)
    below = lax.ppermute(cot[:, :1], "tile", down)
    ends = jnp.concatenate([above, cot, below], axis=1)
    last, first = ends[:, :, COLS - 1 :], ends[:, :, :1]
    before = lax.ppermute(last, "face", [(i, (i + 1) % 4) for i in range(4)])
    after = lax.ppermute(first, "face", [((i + 1) % 4, i) for i in range(4)])
    gap = jnp.zeros((HID, ROWS + 2, PP - 2), bf16)
    side = jnp.concatenate([after, gap, before], axis=2).transpose(1, 0, 2)
    rim = jnp.concatenate([above, below], axis=1).transpose(1, 0, 2)
    return cot.transpose(1, 0, 2), rim, side


def local(latlon, intersection_weight, target_dev, target_piece, counts, conv_weight, cotangent):
    blocks = latlon.shape[0]
    owners = jnp.arange(DEVS, dtype=jnp.int32)
    live = (jnp.arange(K, dtype=jnp.int32)[None, :] < counts[:, None]).astype(jnp.int32)
    entry = jnp.arange(blocks * K, dtype=jnp.int32).reshape(blocks, K)
    code = (entry * 64 + target_piece) * 2 + live
    mine = target_dev[None] == owners[:, None, None]
    first = jnp.min(jnp.where(mine, code[None], jnp.int32(1 << 24)), axis=(1, 2))
    second = jnp.max(jnp.where(mine, code[None], jnp.int32(-1)), axis=(1, 2))
    keys = jnp.stack([first, second], axis=1).reshape(-1)
    flat = target_dev.reshape(-1)
    order = entry.reshape(-1)
    slot = jnp.sum(
        ((flat[:, None] == flat[None, :]) & (order[None, :] < order[:, None])).astype(jnp.int32),
        axis=1,
    )
    places = flat * 4 + slot * 2 + live.reshape(-1)

    cots = cotangent_rim(cotangent[0])
    send = partial_products(
        keys, latlon.transpose(1, 0, 2), intersection_weight.reshape(blocks * K, PP, PP)
    )
    recv = exchange(send)
    pieces = jnp.stack([recv[:, C, 0], recv[:, SL + C, 0]], axis=1).reshape(-1).astype(jnp.int32)
    field, pack = gather_field(pieces, recv)
    top, bottom, side = halo(field, pack)

    kernel = conv_weight.reshape(3, 3, HID, C)
    kernel = jnp.pad(kernel, ((0, 0), (0, 0), (0, 0), (0, CP - C)))
    wf = kernel.transpose(0, 2, 1, 3).reshape(3, HID, 3 * CP)
    wb = kernel.transpose(0, 1, 3, 2).reshape(3, 3 * CP, HID)
    meta = lax.axis_index("tile").astype(jnp.int32).reshape(1)
    act, rows, dfield = conv(meta, field, top, bottom, side, wf, wb, cots)
    reply = replies(pieces, dfield, rows)
    activation = channel_major(act)[None]
    back = exchange(reply)
    share = jnp.sum(back[:, 2 * C : 2 * C + SHARE].astype(f32), axis=0)
    share = (share * (1.0 / math.sqrt(DEVS * ROWS * COLS))).astype(bf16)
    summed = exchange(jnp.broadcast_to(share[None], (DEVS, SHARE, PP)))
    summed = summed.reshape(DEVS * SHARE, PP)[: 18 * C].reshape(2, 9, C, PP)
    grad_conv = summed.astype(f32).transpose(1, 0, 3, 2).reshape(9, HID, C)
    grad_latlon = final_products(places, back, intersection_weight).transpose(1, 0, 2)
    return (activation, grad_conv, grad_latlon)


def solution(mesh):
    placed = (
        P(("face", "tile"), None, None),
        P(("face", "tile"), None, None, None),
        P(("face", "tile"), None),
        P(("face", "tile"), None),
        P(("face", "tile")),
        P(),
        P("face", None, "tile", None),
    )
    return jax.shard_map(
        local,
        mesh=mesh,
        in_specs=placed,
        out_specs=(P("face", None, "tile", None), P(), P(("face", "tile"), None, None)),
        check_vma=False,
    )
```
